32 devices in a mesh: row: 8 (over z, y), col: 4 (over x, core).
Axes of the slice: x: 2, y: 2, z: 4, core: 2. Of those that a mesh axis runs over, the one named last changes fastest.
Arguments:
- tile_u: bfloat16 [3, 8, 2, 4, 512, 128], P(None, 'row', None, 'col'), may hold values from -6 to 6
- tile_v: bfloat16 [3, 8, 2, 4, 512, 128], P(None, 'row', None, 'col'), may hold values from -6 to 6
- tile_ranks: int32 [3, 8, 2, 4], P(None, 'row', None, 'col'), may hold values from 16 to 128
- lower_inverse: bfloat16 [2, 512, 512], replicated, as said below
- upper_inverse: bfloat16 [2, 512, 512], replicated, as said below
- row_order: int32 [2, 512], replicated, may hold values from 0 to 511, each once within a row
- sketch: bfloat16 [512, 128], replicated, may hold values from -0.25 to 0.25
Outputs:
- new_u: bfloat16 [3, 8, 2, 4, 512, 128], P(None, 'row', None, 'col')
- new_v: bfloat16 [3, 8, 2, 4, 512, 128], P(None, 'row', None, 'col')
The draws below stay inside these ranges and needn't reach their ends.
Inputs may be any that keep to these rules, and one draw needn't show every extreme that they name: Each row of row_order names every number of 0 to 511 once. Each lower_inverse[k] is lower triangular with a unit diagonal. Each upper_inverse[k] is upper triangular with a positive diagonal.
All inputs are finite; a program needn't handle non-finite values.
Results may differ from the reference program's by a relative error of at most 0.03.
Values may be sent and summed in bfloat16 or wider, within the bound.
A program may use at most 64 MiB of HBM per device.

```python
import math
import jax
import jax.numpy as jnp
from jax import lax

B = 512
R = 128
PANELS = 2
TR_DEV = 3
TC_DEV = 2
N_ROW = 8
N_COL = 4


def draw_lower_inverse(key, part):
    noise = jax.random.normal(key, (PANELS, B, B), jnp.float32)
    strict = jnp.tril(noise, -1) * B ** (-0.5)
    return (strict + jnp.eye(B, dtype=jnp.float32)).astype(jnp.bfloat16)


def draw_upper_inverse(key, part):
    first_key, second_key = jax.random.split(jax.random.fold_in(key, 7))
    noise = jax.random.normal(first_key, (PANELS, B, B), jnp.float32)
    diagonal = jnp.exp(jax.random.uniform(second_key, (PANELS, B), jnp.float32, math.log(0.5), math.log(2.0)))
    matrix = jnp.triu(noise, 1) * B ** (-0.5) + diagonal[:, :, None] * jnp.eye(B, dtype=jnp.float32)
    return (matrix * B ** (-0.5)).astype(jnp.bfloat16)


def with_ends(values, key, low, largest):
    longest = values.shape.index(max(values.shape))
    spots = []
    for shift in (0, 1):
        where = [jax.random.randint(jax.random.fold_in(key, axis), (), 0, length) for axis, length in enumerate(values.shape)]
        where[longest] = (where[longest] + shift) % values.shape[longest]
        spots.append(tuple(where))
    return values.at[spots[0]].set(low).at[spots[1]].set(largest)


def level_of(rng, shape, cuts, least, top_value):
    def one(position, blocks):
        steps = jax.random.uniform(jax.random.fold_in(jax.random.fold_in(rng, 6), position), (blocks,), jnp.float32, least / len(cuts), top_value / len(cuts))
        return jnp.repeat(jnp.exp(steps), shape[position] // blocks).reshape((-1,) + (1,) * (len(shape) - position - 1))

    factor_of = one(*cuts[0])
    for cut in cuts[1:]:
        factor_of = factor_of * one(*cut)
    return factor_of


def scatter_about(stream_key, shape, scale, bound, cuts=(), held_as=jnp.bfloat16):
    drawn = jax.random.normal(stream_key, shape, jnp.float32) * scale
    if len(cuts) > 0:
        drawn = level_of(stream_key, shape, cuts, -0.22, 0.18) * drawn
    return jnp.clip(drawn, min=-bound, max=bound).astype(held_as)


def setup_inputs(seed: int = 0) -> dict:
    key_of = jax.random.split(jax.random.key(seed), 8)
    tile_u = scatter_about(key_of[0], (TR_DEV, N_ROW, TC_DEV, N_COL, B, R), 1.0, 6.0, ((1, 8), (3, 4)))
    tile_v = scatter_about(key_of[1], (TR_DEV, N_ROW, TC_DEV, N_COL, B, R), 1.0, 6.0, ((1, 8), (3, 4)))
    tile_ranks = with_ends(jax.random.randint(key_of[2], (TR_DEV, N_ROW, TC_DEV, N_COL), R // 8, R + 1), jax.random.fold_in(key_of[2], 1), R // 8, R).astype(jnp.int32)
    lower_inverse = draw_lower_inverse(jax.random.fold_in(key_of[7], 71), 0)
    upper_inverse = draw_upper_inverse(jax.random.fold_in(key_of[7], 71), 0)
    row_order = jax.vmap(lambda own: jax.random.permutation(own, B))(jax.random.split(key_of[5], PANELS)).reshape((PANELS, B)).astype(jnp.int32)
    sketch = scatter_about(key_of[6], (B, R), B ** -0.5, 0.25)
    return dict(tile_u=tile_u, tile_v=tile_v, tile_ranks=tile_ranks, lower_inverse=lower_inverse, upper_inverse=upper_inverse, row_order=row_order, sketch=sketch)


HIGHEST = lax.Precision.HIGHEST

def compress(tile_uf, tile_vf, left_u, coupling, top_v, keep_cols, sketch):
    rank_width = tile_uf.shape[-1]
    tile_size = tile_uf.shape[-2]
    product = jnp.einsum('...br,...rs->...bs', left_u.astype(jnp.float32), coupling.astype(jnp.float32), precision=HIGHEST)
    update = (product * rank_width ** (-0.5)).astype(jnp.bfloat16)
    stacked_left = jnp.concatenate([tile_uf, -update], axis=-1).astype(jnp.float32)
    stacked_right = jnp.concatenate([tile_vf, top_v], axis=-1).astype(jnp.float32)
    probe_mat = jnp.einsum('...bt,br->...tr', stacked_right, sketch.astype(jnp.float32), precision=HIGHEST)
    sample = jnp.einsum('...bt,...tr->...br', stacked_left, probe_mat, precision=HIGHEST) * keep_cols[..., None, :]
    gram_matrix = jnp.einsum('...br,...bs->...rs', sample, sample, precision=HIGHEST)
    gram_matrix = gram_matrix + (1.0 - keep_cols)[..., :, None] * jnp.eye(rank_width, dtype=jnp.float32)
    factor = jnp.linalg.cholesky(gram_matrix)
    solved = lax.linalg.triangular_solve(factor, jnp.swapaxes(sample, -1, -2), left_side=True, lower=True)
    new_basis = jnp.swapaxes(solved, -1, -2)
    weights_q = jnp.einsum('...bt,...br->...tr', stacked_left, new_basis, precision=HIGHEST)
    fresh_v = jnp.einsum('...bt,...tr->...br', stacked_right, weights_q, precision=HIGHEST)
    return ((new_basis * tile_size ** 0.5).astype(jnp.bfloat16), (fresh_v * tile_size ** (-0.5)).astype(jnp.bfloat16))

def reference(tile_u, tile_v, tile_ranks, lower_inverse, upper_inverse, row_order, sketch):
    tile_rows = TR_DEV * N_ROW
    tile_cols = TC_DEV * N_COL
    shape_four = (tile_rows, tile_cols, B, R)
    tile_rank = tile_ranks.reshape(tile_rows, tile_cols)
    keep_flags_mask = jnp.arange(R, dtype=jnp.int32)[None, None, :] < tile_rank[:, :, None]
    keep_cols = keep_flags_mask.astype(jnp.float32)
    keep_half = keep_flags_mask.astype(jnp.bfloat16)[:, :, None, :]
    factor_left_bases = tile_u.reshape(shape_four) * keep_half
    factors_v = tile_v.reshape(shape_four) * keep_half
    row_ids = jnp.arange(tile_rows, dtype=jnp.int32)
    col_ids = jnp.arange(tile_cols, dtype=jnp.int32)
    for panel in range(PANELS):
        permuted = jnp.take(factor_left_bases[panel], row_order[panel], axis=1)
        turned_u = jnp.einsum('ab,mbr->mar', lower_inverse[panel].astype(jnp.float32), permuted.astype(jnp.float32), precision=HIGHEST).astype(jnp.bfloat16)
        top_u = jnp.where((col_ids > panel)[:, None, None], turned_u, factor_left_bases[panel])
        transposed_right_basis = jnp.einsum('ba,lbr->lar', upper_inverse[panel].astype(jnp.float32), factors_v[:, panel].astype(jnp.float32), precision=HIGHEST)
        transposed_right_basis = (transposed_right_basis * B ** 0.5).astype(jnp.bfloat16)
        left_right_basis = jnp.where((row_ids > panel)[:, None, None], transposed_right_basis, factors_v[:, panel])
        factor_left_bases = factor_left_bases.at[panel].set(top_u)
        factors_v = factors_v.at[:, panel].set(left_right_basis)
        top_v = factors_v[panel]
        left_u = factor_left_bases[:, panel]

        def single_row_slice(row_item, panel=panel, top_u=top_u, top_v=top_v):
            row_u, row_v, row_left_u, row_left_v, row_keep, row_id = row_item
            coupling = jnp.einsum('br,mbs->mrs', row_left_v.astype(jnp.float32), top_u.astype(jnp.float32), precision=HIGHEST)
            coupling = (coupling * B ** (-0.5)).astype(jnp.bfloat16)
            left_full = jnp.broadcast_to(row_left_u[None], row_u.shape)
            fresh_u, fresh_v = compress(row_u, row_v, left_full, coupling, top_v, row_keep, sketch)
            chosen = ((row_id > panel) & (col_ids > panel))[:, None, None]
            return (jnp.where(chosen, fresh_u, row_u), jnp.where(chosen, fresh_v, row_v))
        factor_left_bases, factors_v = lax.map(single_row_slice, (factor_left_bases, factors_v, left_u, left_right_basis, keep_cols, row_ids))
    return (factor_left_bases.reshape(tile_u.shape), factors_v.reshape(tile_v.shape))
```

```python
import functools

import jax
import jax.numpy as jnp
from jax import lax
from jax.experimental import pallas as pl
from jax.experimental.pallas import tpu as pltpu
from jax.sharding import PartitionSpec as P

PANELS = 2
GROUP = 8
BLOCK = 32
F32 = jnp.float32
BF16 = jnp.bfloat16

NN = (((1,), (0,)), ((), ()))
NT = (((1,), (1,)), ((), ()))
TN = (((0,), (0,)), ((), ()))


def mm(left, right, dims=NN):
    return lax.dot_general(left, right, dims, preferred_element_type=F32)


def halves(value):
    high = value.astype(BF16)
    low = (value - high.astype(F32)).astype(BF16)
    return high, low


def inverse_factor(gram):
    tiles, size, _ = gram.shape
    lane = lax.broadcasted_iota(jnp.int32, (1, 1, size), 2)
    sub = lax.broadcasted_iota(jnp.int32, (1, GROUP, 1), 1)
    below = gram
    done = []
    for first in range(0, size, BLOCK):
        groups = [
            below[:, at : at + GROUP, :] for at in range(0, BLOCK, GROUP)
        ]
        scales = []
        for step in range(BLOCK):
            pivot = first + step
            home, line = divmod(step, GROUP)
            own = groups[home]
            row = own[:, line : line + 1, :]
            inverse = 1.0 / row[:, :, pivot : pivot + 1]
            at_pivot = lane == pivot
            turned = jnp.where(at_pivot, 1.0, row) * inverse
            for g in range(home, BLOCK // GROUP):
                value = groups[g]
                column = value[:, :, pivot : pivot + 1]
                fresh = jnp.where(at_pivot, 0.0, value) - column * turned
                groups[g] = jnp.where(sub > line, fresh, value) if g == home else fresh
        block = jnp.concatenate(groups, axis=1)
        row_id = first + lax.broadcasted_iota(jnp.int32, (1, BLOCK, 1), 1)
        diagonal = jnp.sum(jnp.where(lane == row_id, block, 0.0), axis=2, keepdims=True)
        block = jnp.where(lane == row_id, 1.0, block) * lax.rsqrt(diagonal)
        inner = (lane >= first) & (lane < first + BLOCK)
        block = jnp.where(inner & (lane > row_id), 0.0, block)
        done.append(jnp.where(lane > row_id, 0.0, block))
        if first + BLOCK < size:
            rest = below[:, BLOCK:, :]
            parts = []
            for t in range(tiles):
                spread = block[t].T[first + BLOCK :, :]
                parts.append(
                    jnp.where(inner[0], 0.0, rest[t])
                    - lax.dot_general(
                        spread,
                        block[t],
                        NN,
                        precision=lax.Precision.HIGHEST,
                        preferred_element_type=F32,
                    )
                )
            below = jnp.stack(parts)
    return jnp.concatenate(done, axis=1)


def panel_kernel(
    panel,
    row_size,
    col_size,
    ranks_ref,
    u_ref,
    v_ref,
    top_u_ref,
    top_v_ref,
    left_u_ref,
    left_v_ref,
    lower_ref,
    upper_ref,
    order_ref,
    sketch_ref,
    out_u_ref,
    out_v_ref,
    turned_ref,
    side_ref,
    x_ref,
    s_ref,
):
    row_tiles, col_tiles, tile_size, rank_width = u_ref.shape
    rows = [lax.axis_index("row") + a * row_size for a in range(row_tiles)]
    cols = [lax.axis_index("col") + e * col_size for e in range(col_tiles)]
    tiles = [(a, e) for a in range(row_tiles) for e in range(col_tiles)]

    place = lax.broadcasted_iota(jnp.int32, (tile_size, tile_size), 1)
    chosen = jnp.where(order_ref[...] == place, 1.0, 0.0).astype(BF16)
    for e in range(col_tiles):
        raw = top_u_ref[e]
        permuted = mm(chosen, raw).astype(BF16)
        turned = mm(lower_ref[...], permuted).astype(BF16)
        turned_ref[e] = jnp.where(cols[e] > panel, turned, raw)
    for a in range(row_tiles):
        raw = left_v_ref[a]
        turned = (mm(upper_ref[...], raw, TN) * tile_size**0.5).astype(BF16)
        side_ref[a] = jnp.where(rows[a] > panel, turned, raw)

    sketch = sketch_ref[...]
    top_probe = [mm(sketch, top_v_ref[e], TN) for e in range(col_tiles)]
    row_at = lax.broadcasted_iota(jnp.int32, (rank_width, 1), 0)
    diag = row_at == lax.broadcasted_iota(jnp.int32, (rank_width, rank_width), 1)
    grams = []
    for t, (a, e) in enumerate(tiles):
        coupling = (mm(side_ref[a], turned_ref[e], TN) * tile_size**-0.5).astype(BF16)
        update = (mm(left_u_ref[a], coupling) * rank_width**-0.5).astype(BF16)
        x = jnp.concatenate([u_ref[a, e], -update], axis=1)
        x_ref[t] = x
        probe = jnp.concatenate([mm(sketch, v_ref[a, e], TN), top_probe[e]], axis=1)
        keep = row_at < ranks_ref[t]
        probe = jnp.where(keep, probe, 0.0)
        high, low = halves(probe)
        sample = mm(high, x, NT) + mm(low, x, NT)
        s_ref[t] = sample
        high, low = halves(sample)
        cross = mm(high, low, NT)
        gram = mm(high, high, NT) + (cross + cross.T)
        grams.append(gram + jnp.where(diag & ~keep, 1.0, 0.0))
    inverse = inverse_factor(jnp.stack(grams))
    for t, (a, e) in enumerate(tiles):
        high, low = halves(inverse[t])
        s_high, s_low = halves(s_ref[t])
        basis = mm(high, s_high) + (mm(high, s_low) + mm(low, s_high))
        fresh_u = (basis * tile_size**0.5).T.astype(BF16)
        x = x_ref[t]
        high, low = halves(basis)
        weights = mm(high, x) + mm(low, x)
        w_high, w_low = halves(weights)
        y = jnp.concatenate([v_ref[a, e], top_v_ref[e]], axis=1)
        fresh_v = ((mm(y, w_high, NT) + mm(y, w_low, NT)) * tile_size**-0.5).astype(BF16)
        old_u, old_v = u_ref[a, e], v_ref[a, e]
        if a == 0:
            old_u = jnp.where(rows[a] == panel, turned_ref[e], old_u)
        if e == 0:
            old_v = jnp.where(cols[e] == panel, side_ref[a], old_v)
        active = (rows[a] > panel) & (cols[e] > panel)
        out_u_ref[a, e] = jnp.where(active, fresh_u, old_u)
        out_v_ref[a, e] = jnp.where(active, fresh_v, old_v)


def from_root(array, axis, root):
    mine = lax.axis_index(axis) == root
    return lax.psum(jnp.where(mine, array, jnp.zeros_like(array)), axis)


def on_device(
    row_size, col_size, tile_u, tile_v, tile_ranks, lower_inverse, upper_inverse, row_order, sketch
):
    row_tiles, col_tiles = tile_u.shape[0], tile_u.shape[2]
    tile_size, rank_width = tile_u.shape[4], tile_u.shape[5]
    shape_four = (row_tiles, col_tiles, tile_size, rank_width)
    ranks = tile_ranks.reshape(row_tiles, col_tiles)
    keep = (jnp.arange(rank_width, dtype=jnp.int32) < ranks[:, :, None]).astype(BF16)
    u = tile_u.reshape(shape_four) * keep[:, :, None, :]
    v = tile_v.reshape(shape_four) * keep[:, :, None, :]
    ranks = ranks.reshape(-1)
    tiles = row_tiles * col_tiles
    vmem = pl.BlockSpec(memory_space=pltpu.VMEM)
    for panel in range(PANELS):
        top = from_root(jnp.stack([u[0], v[0]]), "row", panel)
        left = from_root(jnp.stack([u[:, 0], v[:, 0]]), "col", panel)
        u, v = pl.pallas_call(
            functools.partial(panel_kernel, panel, row_size, col_size),
            out_shape=(
                jax.ShapeDtypeStruct(shape_four, BF16),
                jax.ShapeDtypeStruct(shape_four, BF16),
            ),
            in_specs=[pl.BlockSpec(memory_space=pltpu.SMEM)] + [vmem] * 10,
            out_specs=(vmem, vmem),
            scratch_shapes=[
                pltpu.VMEM((col_tiles, tile_size, rank_width), BF16),
                pltpu.VMEM((row_tiles, tile_size, rank_width), BF16),
                pltpu.VMEM((tiles, tile_size, 2 * rank_width), BF16),
                pltpu.VMEM((tiles, rank_width, tile_size), F32),
            ],
            name=f"panel_{panel}",
        )(
            ranks,
            u,
            v,
            top[0],
            top[1],
            left[0],
            left[1],
            lower_inverse[panel],
            upper_inverse[panel],
            row_order[panel].reshape(tile_size, 1),
            sketch,
        )
    return u.reshape(tile_u.shape), v.reshape(tile_v.shape)


def solution(mesh):
    tile_spec = P(None, "row", None, "col", None, None)
    return jax.shard_map(
        functools.partial(on_device, mesh.shape["row"], mesh.shape["col"]),
        mesh=mesh,
        in_specs=(tile_spec, tile_spec, P(None, "row", None, "col"), P(), P(), P(), P()),
        out_specs=(tile_spec, tile_spec),
        check_vma=False,
    )
```

```python
import functools

import jax
import jax.numpy as jnp
from jax import lax
from jax.experimental import pallas as pl
from jax.experimental.pallas import tpu as pltpu
from jax.sharding import PartitionSpec as P

PANELS = 2
GROUP = 8
BLOCK = 32
CHUNKS = 4
F32 = jnp.float32
BF16 = jnp.bfloat16

NN = (((1,), (0,)), ((), ()))
NT = (((1,), (1,)), ((), ()))
TN = (((0,), (0,)), ((), ()))


def mm(left, right, dims=NN):
    return lax.dot_general(left, right, dims, preferred_element_type=F32)


def halves(value):
    high = value.astype(BF16)
    low = (value - high.astype(F32)).astype(BF16)
    return high, low


def inverse_factor(gram):
    tiles, size, _ = gram.shape
    lane = lax.broadcasted_iota(jnp.int32, (1, 1, size), 2)
    sub = lax.broadcasted_iota(jnp.int32, (1, GROUP, 1), 1)
    below = gram
    done = []
    for first in range(0, size, BLOCK):
        groups = [
            below[:, at : at + GROUP, :] for at in range(0, BLOCK, GROUP)
        ]
        scales = []
        for step in range(BLOCK):
            pivot = first + step
            home, line = divmod(step, GROUP)
            own = groups[home]
            row = own[:, line : line + 1, :]
            inverse = 1.0 / row[:, :, pivot : pivot + 1]
            at_pivot = lane == pivot
            turned = jnp.where(at_pivot, 1.0, row) * inverse
            for g in range(home, BLOCK // GROUP):
                value = groups[g]
                column = value[:, :, pivot : pivot + 1]
                fresh = jnp.where(at_pivot, 0.0, value) - column * turned
                groups[g] = jnp.where(sub > line, fresh, value) if g == home else fresh
        block = jnp.concatenate(groups, axis=1)
        row_id = first + lax.broadcasted_iota(jnp.int32, (1, BLOCK, 1), 1)
        diagonal = jnp.sum(jnp.where(lane == row_id, block, 0.0), axis=2, keepdims=True)
        block = jnp.where(lane == row_id, 1.0, block) * lax.rsqrt(diagonal)
        inner = (lane >= first) & (lane < first + BLOCK)
        block = jnp.where(inner & (lane > row_id), 0.0, block)
        done.append(jnp.where(lane > row_id, 0.0, block))
        if first + BLOCK < size:
            rest = below[:, BLOCK:, :]
            parts = []
            for t in range(tiles):
                spread = block[t].T[first + BLOCK :, :]
                parts.append(
                    jnp.where(inner[0], 0.0, rest[t])
                    - lax.dot_general(
                        spread,
                        block[t],
                        NN,
                        precision=lax.Precision.HIGHEST,
                        preferred_element_type=F32,
                    )
                )
            below = jnp.stack(parts)
    return jnp.concatenate(done, axis=1)


class Tree:
    def __init__(self, axis, size, root):
        place = lax.axis_index(axis)
        self.axis = axis
        self.pair = place + 1 - 2 * lax.rem(place, 2)
        self.chain = lax.rem(place, 2) == root
        self.is_root = place == root
        self.has_next = self.chain & (place + 2 < size)
        self.next = jnp.minimum(place + 2, size - 1)
        self.parent = jnp.where(self.chain, jnp.maximum(place - 2, 0), self.pair)
        self.place = place

    def greet(self, barrier):
        @pl.when(~self.is_root)
        def _():
            self.signal(barrier, self.parent)

        @pl.when(self.chain)
        def _():
            self.signal(barrier, self.pair)

        @pl.when(self.has_next)
        def _():
            self.signal(barrier, self.next)

    def signal(self, barrier, place):
        pl.semaphore_signal(
            barrier, inc=1, device_id={self.axis: place}, device_id_type=pl.DeviceIdType.MESH
        )

    def met(self):
        return (
            (~self.is_root).astype(jnp.int32)
            + self.chain.astype(jnp.int32)
            + self.has_next.astype(jnp.int32)
        )

    def copy(self, source, target, send_sem, recv_sem, place):
        return pltpu.make_async_remote_copy(
            src_ref=source,
            dst_ref=target,
            send_sem=send_sem,
            recv_sem=recv_sem,
            device_id={self.axis: place},
            device_id_type=pl.DeviceIdType.MESH,
        )

    def send(self, source, target, sends, recv, c):
        @pl.when(self.has_next)
        def _():
            self.copy(source, target, sends.at[c, 0], recv.at[c], self.next).start()

        @pl.when(self.chain)
        def _():
            self.copy(source, target, sends.at[c, 1], recv.at[c], self.pair).start()

    def sent(self, target, sends, recv, c):
        @pl.when(self.has_next)
        def _():
            self.copy(target, target, sends.at[c, 0], recv.at[c], self.next).wait_send()

        @pl.when(self.chain)
        def _():
            self.copy(target, target, sends.at[c, 1], recv.at[c], self.pair).wait_send()

    def received(self, target, sends, recv, c):
        self.copy(target, target, sends.at[c, 0], recv.at[c], self.parent).wait_recv()


def panels_kernel(
    row_size,
    col_size,
    ranks_ref,
    u_ref,
    v_ref,
    lower_ref,
    upper_ref,
    order_ref,
    sketch_ref,
    out_u_ref,
    out_v_ref,
    top_ref,
    left_ref,
    moved_ref,
    turned_ref,
    side_ref,
    x_ref,
    s_ref,
    top_send,
    top_recv,
    left_send,
    left_recv,
):
    row_tiles, col_tiles, tile_size, rank_width = u_ref.shape
    rows = [lax.axis_index("row") + a * row_size for a in range(row_tiles)]
    cols = [lax.axis_index("col") + e * col_size for e in range(col_tiles)]
    tiles = [(a, e) for a in range(row_tiles) for e in range(col_tiles)]
    early = [t for t, (a, e) in enumerate(tiles) if a == 0 or e == 0]
    late = [t for t, (a, e) in enumerate(tiles) if a > 0 and e > 0]
    piece = tile_size // CHUNKS
    row_trees = [Tree("row", row_size, panel) for panel in range(PANELS)]
    col_trees = [Tree("col", col_size, panel) for panel in range(PANELS)]

    barrier = pltpu.get_barrier_semaphore()
    met = 0
    for tree in row_trees + col_trees:
        tree.greet(barrier)
        met = met + tree.met()
    pl.semaphore_wait(barrier, met)

    def flows(panel):
        u_from, v_from = (u_ref, v_ref) if panel == 0 else (out_u_ref, out_v_ref)
        top, left = [], []
        for which, ref in ((1, v_from), (0, u_from)):
            for q in range(CHUNKS):
                part = pl.ds(q * piece, piece)
                for e in range(col_tiles):
                    top.append((ref.at[0, e, part], top_ref.at[panel, which, e, part]))
                for a in range(row_tiles):
                    left.append((ref.at[a, 0, part], left_ref.at[panel, which, a, part]))
        return [
            (row_trees[panel], top, top_send.at[panel], top_recv.at[panel]),
            (col_trees[panel], left, left_send.at[panel], left_recv.at[panel]),
        ]

    def launch(panel):
        u_from, v_from = (u_ref, v_ref) if panel == 0 else (out_u_ref, out_v_ref)
        for tree, pieces, sends, recv in flows(panel):

            @pl.when(tree.is_root)
            def _():
                for c, (source, target) in enumerate(pieces):
                    tree.send(source, target, sends, recv, c)

        @pl.when(row_trees[panel].is_root)
        def _():
            top_ref[panel, 0] = u_from[0]
            top_ref[panel, 1] = v_from[0]

        @pl.when(col_trees[panel].is_root)
        def _():
            left_ref[panel, 0] = u_from[:, 0]
            left_ref[panel, 1] = v_from[:, 0]

    def relay(panel):
        pending = [
            (c / len(pieces), which, c)
            for which, (_, pieces, _, _) in enumerate(flows(panel))
            for c in range(len(pieces))
        ]
        for _, which, c in sorted(pending):
            tree, pieces, sends, recv = flows(panel)[which]
            target = pieces[c][1]

            @pl.when(~tree.is_root)
            def _():
                tree.received(target, sends, recv, c)
                tree.send(target, target, sends, recv, c)

    def settle(panel):
        for tree, pieces, sends, recv in flows(panel):
            for c, (_, target) in enumerate(pieces):
                tree.sent(target, sends, recv, c)

    launch(0)
    place = lax.broadcasted_iota(jnp.int32, (tile_size, tile_size), 0)
    for panel in range(PANELS):
        chosen = jnp.where(order_ref[panel : panel + 1, :] == place, 1.0, 0.0).astype(BF16)
        moved_ref[panel] = mm(lower_ref[panel], chosen, NT).astype(BF16)

    row_at = lax.broadcasted_iota(jnp.int32, (rank_width, 1), 0)
    diag = row_at == lax.broadcasted_iota(jnp.int32, (rank_width, rank_width), 1)
    sketch = sketch_ref[...]
    for panel in range(PANELS):
        from_u, from_v = (u_ref, v_ref) if panel == 0 else (out_u_ref, out_v_ref)
        relay(panel)
        for e in range(col_tiles):
            raw = top_ref[panel, 0, e]
            turned = mm(moved_ref[panel], raw).astype(BF16)
            turned_ref[e] = jnp.where(cols[e] > panel, turned, raw)
        for a in range(row_tiles):
            raw = left_ref[panel, 1, a]
            turned = (mm(upper_ref[panel], raw, TN) * tile_size**0.5).astype(BF16)
            side_ref[a] = jnp.where(rows[a] > panel, turned, raw)

        top_probe = [mm(sketch, top_ref[panel, 1, e], TN) for e in range(col_tiles)]
        grams = []
        for t, (a, e) in enumerate(tiles):
            coupling = (mm(side_ref[a], turned_ref[e], TN) * tile_size**-0.5).astype(BF16)
            update = (mm(left_ref[panel, 0, a], coupling) * rank_width**-0.5).astype(BF16)
            x = jnp.concatenate([from_u[a, e], -update], axis=1)
            x_ref[t] = x
            probe = jnp.concatenate([mm(sketch, from_v[a, e], TN), top_probe[e]], axis=1)
            keep = row_at < ranks_ref[t]
            probe = jnp.where(keep, probe, 0.0)
            high, low = halves(probe)
            sample = mm(high, x, NT) + mm(low, x, NT)
            s_ref[t] = sample
            high, low = halves(sample)
            cross = mm(high, low, NT)
            gram = mm(high, high, NT) + (cross + cross.T)
            grams.append(gram + jnp.where(diag & ~keep, 1.0, 0.0))
        inverse = inverse_factor(jnp.stack(grams))
        settle(panel)
        for spot, t in enumerate(early + late):
            a, e = tiles[t]
            high, low = halves(inverse[t])
            s_high, s_low = halves(s_ref[t])
            basis = mm(high, s_high) + (mm(high, s_low) + mm(low, s_high))
            fresh_u = (basis * tile_size**0.5).T.astype(BF16)
            x = x_ref[t]
            high, low = halves(basis)
            weights = mm(high, x) + mm(low, x)
            w_high, w_low = halves(weights)
            old_u, old_v = from_u[a, e], from_v[a, e]
            y = jnp.concatenate([old_v, top_ref[panel, 1, e]], axis=1)
            fresh_v = ((mm(y, w_high, NT) + mm(y, w_low, NT)) * tile_size**-0.5).astype(BF16)
            if a == 0:
                old_u = jnp.where(rows[a] == panel, turned_ref[e], old_u)
            if e == 0:
                old_v = jnp.where(cols[e] == panel, side_ref[a], old_v)
            active = (rows[a] > panel) & (cols[e] > panel)
            out_u_ref[a, e] = jnp.where(active, fresh_u, old_u)
            out_v_ref[a, e] = jnp.where(active, fresh_v, old_v)
            if spot == len(early) - 1 and panel + 1 < PANELS:
                launch(panel + 1)


def on_device(
    row_size, col_size, tile_u, tile_v, tile_ranks, lower_inverse, upper_inverse, row_order, sketch
):
    row_tiles, col_tiles = tile_u.shape[0], tile_u.shape[2]
    tile_size, rank_width = tile_u.shape[4], tile_u.shape[5]
    shape_four = (row_tiles, col_tiles, tile_size, rank_width)
    ranks = tile_ranks.reshape(row_tiles, col_tiles)
    keep = (jnp.arange(rank_width, dtype=jnp.int32) < ranks[:, :, None]).astype(BF16)
    u = tile_u.reshape(shape_four) * keep[:, :, None, :]
    v = tile_v.reshape(shape_four) * keep[:, :, None, :]
    tiles = row_tiles * col_tiles
    vmem = pl.BlockSpec(memory_space=pltpu.VMEM)
    tops, lefts = 2 * col_tiles * CHUNKS, 2 * row_tiles * CHUNKS
    new_u, new_v = pl.pallas_call(
        functools.partial(panels_kernel, row_size, col_size),
        out_shape=(
            jax.ShapeDtypeStruct(shape_four, BF16),
            jax.ShapeDtypeStruct(shape_four, BF16),
        ),
        in_specs=[pl.BlockSpec(memory_space=pltpu.SMEM)] + [vmem] * 6,
        out_specs=(vmem, vmem),
        scratch_shapes=[
            pltpu.VMEM((PANELS, 2, col_tiles, tile_size, rank_width), BF16),
            pltpu.VMEM((PANELS, 2, row_tiles, tile_size, rank_width), BF16),
            pltpu.VMEM((PANELS, tile_size, tile_size), BF16),
            pltpu.VMEM((col_tiles, tile_size, rank_width), BF16),
            pltpu.VMEM((row_tiles, tile_size, rank_width), BF16),
            pltpu.VMEM((tiles, tile_size, 2 * rank_width), BF16),
            pltpu.VMEM((tiles, rank_width, tile_size), F32),
            pltpu.SemaphoreType.DMA((PANELS, tops, 2)),
            pltpu.SemaphoreType.DMA((PANELS, tops)),
            pltpu.SemaphoreType.DMA((PANELS, lefts, 2)),
            pltpu.SemaphoreType.DMA((PANELS, lefts)),
        ],
        compiler_params=pltpu.CompilerParams(collective_id=0, has_side_effects=True),
        name="panels",
    )(ranks.reshape(-1), u, v, lower_inverse, upper_inverse, row_order, sketch)
    return new_u.reshape(tile_u.shape), new_v.reshape(tile_v.shape)


def solution(mesh):
    tile_spec = P(None, "row", None, "col", None, None)
    return jax.shard_map(
        functools.partial(on_device, mesh.shape["row"], mesh.shape["col"]),
        mesh=mesh,
        in_specs=(tile_spec, tile_spec, P(None, "row", None, "col"), P(), P(), P(), P()),
        out_specs=(tile_spec, tile_spec),
        check_vma=False,
    )
```

```python
import functools

import jax
import jax.numpy as jnp
from jax import lax
from jax.experimental import pallas as pl
from jax.experimental.pallas import tpu as pltpu
from jax.sharding import PartitionSpec as P

PANELS = 2
GROUP = 8
BLOCK = 32
CHUNKS = 4
F32 = jnp.float32
BF16 = jnp.bfloat16

NN = (((1,), (0,)), ((), ()))
NT = (((1,), (1,)), ((), ()))
TN = (((0,), (0,)), ((), ()))


def mm(left, right, dims=NN):
    return lax.dot_general(left, right, dims, preferred_element_type=F32)


def halves(value):
    high = value.astype(BF16)
    low = (value - high.astype(F32)).astype(BF16)
    return high, low


def inverse_factor(gram):
    tiles, size, _ = gram.shape
    lane = lax.broadcasted_iota(jnp.int32, (1, 1, size), 2)
    sub = lax.broadcasted_iota(jnp.int32, (1, GROUP, 1), 1)
    below = gram
    done = []
    for first in range(0, size, BLOCK):
        groups = [
            below[:, at : at + GROUP, :] for at in range(0, BLOCK, GROUP)
        ]
        scales = []
        for step in range(BLOCK):
            pivot = first + step
            home, line = divmod(step, GROUP)
            own = groups[home]
            row = own[:, line : line + 1, :]
            inverse = 1.0 / row[:, :, pivot : pivot + 1]
            at_pivot = lane == pivot
            turned = jnp.where(at_pivot, 1.0, row) * inverse
            for g in range(home, BLOCK // GROUP):
                value = groups[g]
                column = value[:, :, pivot : pivot + 1]
                fresh = jnp.where(at_pivot, 0.0, value) - column * turned
                groups[g] = jnp.where(sub > line, fresh, value) if g == home else fresh
        block = jnp.concatenate(groups, axis=1)
        row_id = first + lax.broadcasted_iota(jnp.int32, (1, BLOCK, 1), 1)
        diagonal = jnp.sum(jnp.where(lane == row_id, block, 0.0), axis=2, keepdims=True)
        block = jnp.where(lane == row_id, 1.0, block) * lax.rsqrt(diagonal)
        inner = (lane >= first) & (lane < first + BLOCK)
        block = jnp.where(inner & (lane > row_id), 0.0, block)
        done.append(jnp.where(lane > row_id, 0.0, block))
        if first + BLOCK < size:
            rest = below[:, BLOCK:, :]
            parts = []
            for t in range(tiles):
                spread = block[t].T[first + BLOCK :, :]
                parts.append(
                    jnp.where(inner[0], 0.0, rest[t])
                    - lax.dot_general(
                        spread,
                        block[t],
                        NN,
                        precision=lax.Precision.HIGHEST,
                        preferred_element_type=F32,
                    )
                )
            below = jnp.stack(parts)
    return jnp.concatenate(done, axis=1)


class Tree:
    def __init__(self, axis, size, root, crossed=False):
        place = lax.axis_index(axis)
        self.axis = axis
        self.pair = place + 1 - 2 * lax.rem(place, 2)
        self.is_root = place == root
        self.next = jnp.minimum(place + 2, size - 1)
        before = jnp.maximum(place - 2, 0)
        self.home = lax.rem(place, 2) == root
        if crossed:
            self.chain = ~self.home
            self.has_next = self.chain & (place + 2 < size)
            self.has_pair = (self.chain & (place >= 2)) | self.is_root
            self.parent = jnp.where(self.chain & (place >= 2), before, self.pair)
        else:
            self.chain = self.home
            self.has_next = self.chain & (place + 2 < size)
            self.has_pair = self.chain
            self.parent = jnp.where(self.chain, before, self.pair)

    def greet(self, barrier):
        @pl.when(~self.is_root)
        def _():
            self.signal(barrier, self.parent)

        @pl.when(self.has_pair)
        def _():
            self.signal(barrier, self.pair)

        @pl.when(self.has_next)
        def _():
            self.signal(barrier, self.next)

    def signal(self, barrier, place):
        pl.semaphore_signal(
            barrier, inc=1, device_id={self.axis: place}, device_id_type=pl.DeviceIdType.MESH
        )

    def met(self):
        return (
            (~self.is_root).astype(jnp.int32)
            + self.has_pair.astype(jnp.int32)
            + self.has_next.astype(jnp.int32)
        )

    def copy(self, source, target, send_sem, recv_sem, place):
        return pltpu.make_async_remote_copy(
            src_ref=source,
            dst_ref=target,
            send_sem=send_sem,
            recv_sem=recv_sem,
            device_id={self.axis: place},
            device_id_type=pl.DeviceIdType.MESH,
        )

    def send_next(self, source, target, sends, recv, c):
        @pl.when(self.has_next)
        def _():
            self.copy(source, target, sends.at[c, 0], recv.at[c], self.next).start()

    def send_pair(self, source, target, sends, recv, c):
        @pl.when(self.has_pair)
        def _():
            self.copy(source, target, sends.at[c, 1], recv.at[c], self.pair).start()

    def sent(self, target, sends, recv, c):
        @pl.when(self.has_next)
        def _():
            self.copy(target, target, sends.at[c, 0], recv.at[c], self.next).wait_send()

        @pl.when(self.has_pair)
        def _():
            self.copy(target, target, sends.at[c, 1], recv.at[c], self.pair).wait_send()

    def received(self, target, sends, recv, c):
        self.copy(target, target, sends.at[c, 0], recv.at[c], self.parent).wait_recv()


def panels_kernel(
    row_size,
    col_size,
    ranks_ref,
    u_ref,
    v_ref,
    lower_ref,
    upper_ref,
    order_ref,
    sketch_ref,
    out_u_ref,
    out_v_ref,
    top_ref,
    left_ref,
    moved_ref,
    turned_ref,
    side_ref,
    x_ref,
    s_ref,
    top_send,
    top_recv,
    left_send,
    left_recv,
):
    row_tiles, col_tiles, tile_size, rank_width = u_ref.shape
    rows = [lax.axis_index("row") + a * row_size for a in range(row_tiles)]
    cols = [lax.axis_index("col") + e * col_size for e in range(col_tiles)]
    tiles = [(a, e) for a in range(row_tiles) for e in range(col_tiles)]
    early = [t for t, (a, e) in enumerate(tiles) if a == 0 or e == 0]
    late = [t for t, (a, e) in enumerate(tiles) if a > 0 and e > 0]
    piece = tile_size // CHUNKS
    row_trees = [Tree("row", row_size, panel) for panel in range(PANELS)]
    cross_trees = [Tree("row", row_size, panel, True) for panel in range(PANELS)]
    col_trees = [Tree("col", col_size, panel) for panel in range(PANELS)]

    barrier = pltpu.get_barrier_semaphore()
    met = 0
    for tree in row_trees + cross_trees + col_trees:
        tree.greet(barrier)
        met = met + tree.met()
    pl.semaphore_wait(barrier, met)

    def flows(panel):
        u_from, v_from = (u_ref, v_ref) if panel == 0 else (out_u_ref, out_v_ref)
        top, left = [], []
        for which, ref in ((1, v_from), (0, u_from)):
            for q in range(CHUNKS):
                part = pl.ds(q * piece, piece)
                for e in range(col_tiles):
                    top.append((ref.at[0, e, part], top_ref.at[panel, which, e, part]))
                for a in range(row_tiles):
                    left.append((ref.at[a, 0, part], left_ref.at[panel, which, a, part]))
        straight, crossed, side = [], [], []
        for c, (source, target) in enumerate(top):
            sems = (top_send.at[panel], top_recv.at[panel], c)
            if c % 2 == 0:
                straight.append((row_trees[panel], source, target, sems))
            else:
                crossed.append((cross_trees[panel], source, target, sems))
        for c, (source, target) in enumerate(left):
            sems = (left_send.at[panel], left_recv.at[panel], c)
            side.append((col_trees[panel], source, target, sems))
        return straight, crossed, side

    def launch(panel):
        u_from, v_from = (u_ref, v_ref) if panel == 0 else (out_u_ref, out_v_ref)
        straight, crossed, side = flows(panel)

        @pl.when(row_trees[panel].is_root)
        def _():
            for one, other in zip(straight, crossed):
                one[0].send_next(one[1], one[2], *one[3])
                other[0].send_pair(other[1], other[2], *other[3])
            for tree, source, target, sems in straight:
                tree.send_pair(source, target, *sems)

        @pl.when(col_trees[panel].is_root)
        def _():
            for tree, source, target, sems in side:
                tree.send_next(source, target, *sems)
                tree.send_pair(source, target, *sems)

        @pl.when(row_trees[panel].is_root)
        def _():
            top_ref[panel, 0] = u_from[0]
            top_ref[panel, 1] = v_from[0]

        @pl.when(col_trees[panel].is_root)
        def _():
            left_ref[panel, 0] = u_from[:, 0]
            left_ref[panel, 1] = v_from[:, 0]

    def relay(panel):
        straight, crossed, side = flows(panel)

        def follow(first, last):
            pending = [
                (c / len(pieces), which, piece_of)
                for which, pieces in enumerate((first, side))
                for c, piece_of in enumerate(pieces)
            ]
            pending.sort(key=lambda item: item[:2])
            for tree, _, target, sems in [item[2] for item in pending] + last:

                @pl.when(~tree.is_root)
                def _():
                    tree.received(target, *sems)
                    tree.send_next(target, target, *sems)
                    tree.send_pair(target, target, *sems)

        @pl.when(row_trees[panel].home)
        def _():
            follow(straight, crossed)

        @pl.when(~row_trees[panel].home)
        def _():
            follow(crossed, straight)

    def settle(panel):
        for pieces in flows(panel):
            for tree, _, target, sems in pieces:
                tree.sent(target, *sems)

    launch(0)
    place = lax.broadcasted_iota(jnp.int32, (tile_size, tile_size), 0)
    for panel in range(PANELS):
        chosen = jnp.where(order_ref[panel : panel + 1, :] == place, 1.0, 0.0).astype(BF16)
        moved_ref[panel] = mm(lower_ref[panel], chosen, NT).astype(BF16)

    row_at = lax.broadcasted_iota(jnp.int32, (rank_width, 1), 0)
    diag = row_at == lax.broadcasted_iota(jnp.int32, (rank_width, rank_width), 1)
    sketch = sketch_ref[...]
    for panel in range(PANELS):
        from_u, from_v = (u_ref, v_ref) if panel == 0 else (out_u_ref, out_v_ref)
        relay(panel)
        for e in range(col_tiles):
            raw = top_ref[panel, 0, e]
            turned = mm(moved_ref[panel], raw).astype(BF16)
            turned_ref[e] = jnp.where(cols[e] > panel, turned, raw)
        for a in range(row_tiles):
            raw = left_ref[panel, 1, a]
            turned = (mm(upper_ref[panel], raw, TN) * tile_size**0.5).astype(BF16)
            side_ref[a] = jnp.where(rows[a] > panel, turned, raw)

        top_probe = [mm(sketch, top_ref[panel, 1, e], TN) for e in range(col_tiles)]
        grams = []
        for t, (a, e) in enumerate(tiles):
            coupling = (mm(side_ref[a], turned_ref[e], TN) * tile_size**-0.5).astype(BF16)
            update = (mm(left_ref[panel, 0, a], coupling) * rank_width**-0.5).astype(BF16)
            x = jnp.concatenate([from_u[a, e], -update], axis=1)
            x_ref[t] = x
            probe = jnp.concatenate([mm(sketch, from_v[a, e], TN), top_probe[e]], axis=1)
            keep = row_at < ranks_ref[t]
            probe = jnp.where(keep, probe, 0.0)
            high, low = halves(probe)
            sample = mm(high, x, NT) + mm(low, x, NT)
            s_ref[t] = sample
            high, low = halves(sample)
            cross = mm(high, low, NT)
            gram = mm(high, high, NT) + (cross + cross.T)
            grams.append(gram + jnp.where(diag & ~keep, 1.0, 0.0))
        inverse = inverse_factor(jnp.stack(grams))
        settle(panel)
        for spot, t in enumerate(early + late):
            a, e = tiles[t]
            high, low = halves(inverse[t])
            s_high, s_low = halves(s_ref[t])
            basis = mm(high, s_high) + (mm(high, s_low) + mm(low, s_high))
            fresh_u = (basis * tile_size**0.5).T.astype(BF16)
            x = x_ref[t]
            weights = mm(basis.astype(BF16), x).astype(BF16)
            old_u, old_v = from_u[a, e], from_v[a, e]
            y = jnp.concatenate([old_v, top_ref[panel, 1, e]], axis=1)
            fresh_v = (mm(y, weights, NT) * tile_size**-0.5).astype(BF16)
            if a == 0:
                old_u = jnp.where(rows[a] == panel, turned_ref[e], old_u)
            if e == 0:
                old_v = jnp.where(cols[e] == panel, side_ref[a], old_v)
            active = (rows[a] > panel) & (cols[e] > panel)
            out_u_ref[a, e] = jnp.where(active, fresh_u, old_u)
            out_v_ref[a, e] = jnp.where(active, fresh_v, old_v)
            if spot == len(early) - 1 and panel + 1 < PANELS:
                launch(panel + 1)


def on_device(
    row_size, col_size, tile_u, tile_v, tile_ranks, lower_inverse, upper_inverse, row_order, sketch
):
    row_tiles, col_tiles = tile_u.shape[0], tile_u.shape[2]
    tile_size, rank_width = tile_u.shape[4], tile_u.shape[5]
    shape_four = (row_tiles, col_tiles, tile_size, rank_width)
    ranks = tile_ranks.reshape(row_tiles, col_tiles)
    keep = (jnp.arange(rank_width, dtype=jnp.int32) < ranks[:, :, None]).astype(BF16)
    u = tile_u.reshape(shape_four) * keep[:, :, None, :]
    v = tile_v.reshape(shape_four) * keep[:, :, None, :]
    tiles = row_tiles * col_tiles
    vmem = pl.BlockSpec(memory_space=pltpu.VMEM)
    tops, lefts = 2 * col_tiles * CHUNKS, 2 * row_tiles * CHUNKS
    new_u, new_v = pl.pallas_call(
        functools.partial(panels_kernel, row_size, col_size),
        out_shape=(
            jax.ShapeDtypeStruct(shape_four, BF16),
            jax.ShapeDtypeStruct(shape_four, BF16),
        ),
        in_specs=[pl.BlockSpec(memory_space=pltpu.SMEM)] + [vmem] * 6,
        out_specs=(vmem, vmem),
        scratch_shapes=[
            pltpu.VMEM((PANELS, 2, col_tiles, tile_size, rank_width), BF16),
            pltpu.VMEM((PANELS, 2, row_tiles, tile_size, rank_width), BF16),
            pltpu.VMEM((PANELS, tile_size, tile_size), BF16),
            pltpu.VMEM((col_tiles, tile_size, rank_width), BF16),
            pltpu.VMEM((row_tiles, tile_size, rank_width), BF16),
            pltpu.VMEM((tiles, tile_size, 2 * rank_width), BF16),
            pltpu.VMEM((tiles, rank_width, tile_size), F32),
            pltpu.SemaphoreType.DMA((PANELS, tops, 2)),
            pltpu.SemaphoreType.DMA((PANELS, tops)),
            pltpu.SemaphoreType.DMA((PANELS, lefts, 2)),
            pltpu.SemaphoreType.DMA((PANELS, lefts)),
        ],
        compiler_params=pltpu.CompilerParams(collective_id=0, has_side_effects=True),
        name="panels",
    )(ranks.reshape(-1), u, v, lower_inverse, upper_inverse, row_order, sketch)
    return new_u.reshape(tile_u.shape), new_v.reshape(tile_v.shape)


def solution(mesh):
    tile_spec = P(None, "row", None, "col", None, None)
    return jax.shard_map(
        functools.partial(on_device, mesh.shape["row"], mesh.shape["col"]),
        mesh=mesh,
        in_specs=(tile_spec, tile_spec, P(None, "row", None, "col"), P(), P(), P(), P()),
        out_specs=(tile_spec, tile_spec),
        check_vma=False,
    )
```

```python
import functools

import jax
import jax.numpy as jnp
from jax import lax
from jax.experimental import pallas as pl
from jax.experimental.pallas import tpu as pltpu
from jax.sharding import PartitionSpec as P

PANELS = 2
GROUP = 8
BLOCK = 32
CHUNKS = 4
F32 = jnp.float32
BF16 = jnp.bfloat16

NN = (((1,), (0,)), ((), ()))
NT = (((1,), (1,)), ((), ()))
TN = (((0,), (0,)), ((), ()))


def mm(left, right, dims=NN):
    return lax.dot_general(left, right, dims, preferred_element_type=F32)


def halves(value):
    high = value.astype(BF16)
    low = (value - high.astype(F32)).astype(BF16)
    return high, low


def inverse_factor(gram):
    tiles, size, _ = gram.shape
    lane = lax.broadcasted_iota(jnp.int32, (1, 1, size), 2)
    sub = lax.broadcasted_iota(jnp.int32, (1, GROUP, 1), 1)
    below = gram
    done = []
    for first in range(0, size, BLOCK):
        groups = [
            below[:, at : at + GROUP, :] for at in range(0, BLOCK, GROUP)
        ]
        for step in range(0, BLOCK, 2):
            pivot = first + step
            home, line = divmod(step, GROUP)
            own = groups[home]
            one, two = own[:, line : line + 1, :], own[:, line + 1 : line + 2, :]
            at_one, at_two = lane == pivot, lane == pivot + 1
            lead = two[:, :, pivot : pivot + 1]
            inverse = 1.0 / one[:, :, pivot : pivot + 1]
            ratio = one[:, :, pivot + 1 : pivot + 2] * inverse
            inverse_two = 1.0 / (two[:, :, pivot + 1 : pivot + 2] - lead * ratio)
            turned = jnp.where(at_one, 1.0, one) * inverse
            two = jnp.where(at_one, 0.0, two) - lead * turned
            turned_two = jnp.where(at_two, 1.0, two) * inverse_two
            for g in range(home, BLOCK // GROUP):
                value = groups[g]
                column = value[:, :, pivot : pivot + 1]
                column_two = value[:, :, pivot + 1 : pivot + 2] - column * ratio
                middle = jnp.where(at_one, 0.0, value) - column * turned
                fresh = jnp.where(at_two, 0.0, middle) - column_two * turned_two
                if g == home:
                    middle = jnp.where(sub > line, middle, value)
                    fresh = jnp.where(sub > line + 1, fresh, middle)
                groups[g] = fresh
        block = jnp.concatenate(groups, axis=1)
        row_id = first + lax.broadcasted_iota(jnp.int32, (1, BLOCK, 1), 1)
        diagonal = jnp.sum(jnp.where(lane == row_id, block, 0.0), axis=2, keepdims=True)
        block = jnp.where(lane == row_id, 1.0, block) * lax.rsqrt(diagonal)
        inner = (lane >= first) & (lane < first + BLOCK)
        block = jnp.where(inner & (lane > row_id), 0.0, block)
        done.append(jnp.where(lane > row_id, 0.0, block))
        if first + BLOCK < size:
            rest = below[:, BLOCK:, :]
            parts = []
            for t in range(tiles):
                spread = block[t].T[first + BLOCK :, :]
                parts.append(
                    jnp.where(inner[0], 0.0, rest[t])
                    - lax.dot_general(
                        spread,
                        block[t],
                        NN,
                        precision=lax.Precision.HIGHEST,
                        preferred_element_type=F32,
                    )
                )
            below = jnp.stack(parts)
    return jnp.concatenate(done, axis=1)


class Tree:
    def __init__(self, axis, size, root, crossed=False):
        place = lax.axis_index(axis)
        self.axis = axis
        self.pair = place + 1 - 2 * lax.rem(place, 2)
        self.is_root = place == root
        self.next = jnp.minimum(place + 2, size - 1)
        before = jnp.maximum(place - 2, 0)
        self.home = lax.rem(place, 2) == root
        if crossed:
            self.chain = ~self.home
            self.has_next = self.chain & (place + 2 < size)
            self.has_pair = (self.chain & (place >= 2)) | self.is_root
            self.parent = jnp.where(self.chain & (place >= 2), before, self.pair)
        else:
            self.chain = self.home
            self.has_next = self.chain & (place + 2 < size)
            self.has_pair = self.chain
            self.parent = jnp.where(self.chain, before, self.pair)

    def greet(self, barrier):
        @pl.when(~self.is_root)
        def _():
            self.signal(barrier, self.parent)

        @pl.when(self.has_pair)
        def _():
            self.signal(barrier, self.pair)

        @pl.when(self.has_next)
        def _():
            self.signal(barrier, self.next)

    def signal(self, barrier, place):
        pl.semaphore_signal(
            barrier, inc=1, device_id={self.axis: place}, device_id_type=pl.DeviceIdType.MESH
        )

    def met(self):
        return (
            (~self.is_root).astype(jnp.int32)
            + self.has_pair.astype(jnp.int32)
            + self.has_next.astype(jnp.int32)
        )

    def copy(self, source, target, send_sem, recv_sem, place):
        return pltpu.make_async_remote_copy(
            src_ref=source,
            dst_ref=target,
            send_sem=send_sem,
            recv_sem=recv_sem,
            device_id={self.axis: place},
            device_id_type=pl.DeviceIdType.MESH,
        )

    def send_next(self, source, target, sends, recv, c):
        @pl.when(self.has_next)
        def _():
            self.copy(source, target, sends.at[c, 0], recv.at[c], self.next).start()

    def send_pair(self, source, target, sends, recv, c):
        @pl.when(self.has_pair)
        def _():
            self.copy(source, target, sends.at[c, 1], recv.at[c], self.pair).start()

    def sent(self, target, sends, recv, c):
        @pl.when(self.has_next)
        def _():
            self.copy(target, target, sends.at[c, 0], recv.at[c], self.next).wait_send()

        @pl.when(self.has_pair)
        def _():
            self.copy(target, target, sends.at[c, 1], recv.at[c], self.pair).wait_send()

    def received(self, target, sends, recv, c):
        self.copy(target, target, sends.at[c, 0], recv.at[c], self.parent).wait_recv()


def panels_kernel(
    row_size,
    col_size,
    ranks_ref,
    u_ref,
    v_ref,
    lower_ref,
    upper_ref,
    order_ref,
    sketch_ref,
    out_u_ref,
    out_v_ref,
    top_ref,
    left_ref,
    moved_ref,
    turned_ref,
    side_ref,
    x_ref,
    s_ref,
    top_send,
    top_recv,
    left_send,
    left_recv,
):
    row_tiles, col_tiles, tile_size, rank_width = u_ref.shape
    rows = [lax.axis_index("row") + a * row_size for a in range(row_tiles)]
    cols = [lax.axis_index("col") + e * col_size for e in range(col_tiles)]
    tiles = [(a, e) for a in range(row_tiles) for e in range(col_tiles)]
    early = [t for t, (a, e) in enumerate(tiles) if a == 0 or e == 0]
    late = [t for t, (a, e) in enumerate(tiles) if a > 0 and e > 0]
    piece = tile_size // CHUNKS
    row_trees = [Tree("row", row_size, panel) for panel in range(PANELS)]
    cross_trees = [Tree("row", row_size, panel, True) for panel in range(PANELS)]
    col_trees = [Tree("col", col_size, panel) for panel in range(PANELS)]

    barrier = pltpu.get_barrier_semaphore()
    met = 0
    for tree in row_trees + cross_trees + col_trees:
        tree.greet(barrier)
        met = met + tree.met()
    pl.semaphore_wait(barrier, met)

    def flows(panel):
        u_from, v_from = (u_ref, v_ref) if panel == 0 else (out_u_ref, out_v_ref)
        top, left = [], []
        for which, ref in ((1, v_from), (0, u_from)):
            for q in range(CHUNKS):
                part = pl.ds(q * piece, piece)
                for e in range(col_tiles):
                    top.append((ref.at[0, e, part], top_ref.at[panel, which, e, part]))
                for a in range(row_tiles):
                    left.append((ref.at[a, 0, part], left_ref.at[panel, which, a, part]))
        straight, crossed, side = [], [], []
        for c, (source, target) in enumerate(top):
            sems = (top_send.at[panel], top_recv.at[panel], c)
            if c % 2 == 0:
                straight.append((row_trees[panel], source, target, sems))
            else:
                crossed.append((cross_trees[panel], source, target, sems))
        for c, (source, target) in enumerate(left):
            sems = (left_send.at[panel], left_recv.at[panel], c)
            side.append((col_trees[panel], source, target, sems))
        return straight, crossed, side

    def launch(panel):
        u_from, v_from = (u_ref, v_ref) if panel == 0 else (out_u_ref, out_v_ref)
        straight, crossed, side = flows(panel)

        @pl.when(row_trees[panel].is_root)
        def _():
            for one, other in zip(straight, crossed):
                one[0].send_next(one[1], one[2], *one[3])
                other[0].send_pair(other[1], other[2], *other[3])
            for tree, source, target, sems in straight:
                tree.send_pair(source, target, *sems)

        @pl.when(col_trees[panel].is_root)
        def _():
            for tree, source, target, sems in side:
                tree.send_next(source, target, *sems)
                tree.send_pair(source, target, *sems)

        @pl.when(row_trees[panel].is_root)
        def _():
            top_ref[panel, 0] = u_from[0]
            top_ref[panel, 1] = v_from[0]

        @pl.when(col_trees[panel].is_root)
        def _():
            left_ref[panel, 0] = u_from[:, 0]
            left_ref[panel, 1] = v_from[:, 0]

    def relay(panel):
        straight, crossed, side = flows(panel)

        def follow(first, last):
            pending = [
                (c / len(pieces), which, piece_of)
                for which, pieces in enumerate((first, side))
                for c, piece_of in enumerate(pieces)
            ]
            pending.sort(key=lambda item: item[:2])
            for tree, _, target, sems in [item[2] for item in pending] + last:

                @pl.when(~tree.is_root)
                def _():
                    tree.received(target, *sems)
                    tree.send_next(target, target, *sems)
                    tree.send_pair(target, target, *sems)

        @pl.when(row_trees[panel].home)
        def _():
            follow(straight, crossed)

        @pl.when(~row_trees[panel].home)
        def _():
            follow(crossed, straight)

    def settle(panel):
        for pieces in flows(panel):
            for tree, _, target, sems in pieces:
                tree.sent(target, *sems)

    launch(0)
    place = lax.broadcasted_iota(jnp.int32, (tile_size, tile_size), 0)
    for panel in range(PANELS):
        chosen = jnp.where(order_ref[panel : panel + 1, :] == place, 1.0, 0.0).astype(BF16)
        moved_ref[panel] = mm(lower_ref[panel], chosen, NT).astype(BF16)

    row_at = lax.broadcasted_iota(jnp.int32, (rank_width, 1), 0)
    diag = row_at == lax.broadcasted_iota(jnp.int32, (rank_width, rank_width), 1)
    sketch = sketch_ref[...]
    for panel in range(PANELS):
        from_u, from_v = (u_ref, v_ref) if panel == 0 else (out_u_ref, out_v_ref)
        relay(panel)
        for e in range(col_tiles):
            raw = top_ref[panel, 0, e]
            turned = mm(moved_ref[panel], raw).astype(BF16)
            turned_ref[e] = jnp.where(cols[e] > panel, turned, raw)
        for a in range(row_tiles):
            raw = left_ref[panel, 1, a]
            turned = (mm(upper_ref[panel], raw, TN) * tile_size**0.5).astype(BF16)
            side_ref[a] = jnp.where(rows[a] > panel, turned, raw)

        top_probe = [mm(sketch, top_ref[panel, 1, e], TN) for e in range(col_tiles)]
        grams = []
        for t, (a, e) in enumerate(tiles):
            coupling = (mm(side_ref[a], turned_ref[e], TN) * tile_size**-0.5).astype(BF16)
            update = (mm(left_ref[panel, 0, a], coupling) * rank_width**-0.5).astype(BF16)
            x = jnp.concatenate([from_u[a, e], -update], axis=1)
            x_ref[t] = x
            probe = jnp.concatenate([mm(sketch, from_v[a, e], TN), top_probe[e]], axis=1)
            keep = row_at < ranks_ref[t]
            probe = jnp.where(keep, probe, 0.0)
            high, low = halves(probe)
            sample = mm(high, x, NT) + mm(low, x, NT)
            s_ref[t] = sample
            high, low = halves(sample)
            cross = mm(high, low, NT)
            gram = mm(high, high, NT) + (cross + cross.T)
            grams.append(gram + jnp.where(diag & ~keep, 1.0, 0.0))
        inverse = inverse_factor(jnp.stack(grams))
        settle(panel)
        for spot, t in enumerate(early + late):
            a, e = tiles[t]
            high, low = halves(inverse[t])
            s_high, s_low = halves(s_ref[t])
            basis = mm(high, s_high) + (mm(high, s_low) + mm(low, s_high))
            fresh_u = (basis * tile_size**0.5).T.astype(BF16)
            x = x_ref[t]
            weights = mm(basis.astype(BF16), x).astype(BF16)
            old_u, old_v = from_u[a, e], from_v[a, e]
            y = jnp.concatenate([old_v, top_ref[panel, 1, e]], axis=1)
            fresh_v = (mm(y, weights, NT) * tile_size**-0.5).astype(BF16)
            if a == 0:
                old_u = jnp.where(rows[a] == panel, turned_ref[e], old_u)
            if e == 0:
                old_v = jnp.where(cols[e] == panel, side_ref[a], old_v)
            active = (rows[a] > panel) & (cols[e] > panel)
            out_u_ref[a, e] = jnp.where(active, fresh_u, old_u)
            out_v_ref[a, e] = jnp.where(active, fresh_v, old_v)
            if spot == len(early) - 1 and panel + 1 < PANELS:
                launch(panel + 1)


def on_device(
    row_size, col_size, tile_u, tile_v, tile_ranks, lower_inverse, upper_inverse, row_order, sketch
):
    row_tiles, col_tiles = tile_u.shape[0], tile_u.shape[2]
    tile_size, rank_width = tile_u.shape[4], tile_u.shape[5]
    shape_four = (row_tiles, col_tiles, tile_size, rank_width)
    ranks = tile_ranks.reshape(row_tiles, col_tiles)
    keep = (jnp.arange(rank_width, dtype=jnp.int32) < ranks[:, :, None]).astype(BF16)
    u = tile_u.reshape(shape_four) * keep[:, :, None, :]
    v = tile_v.reshape(shape_four) * keep[:, :, None, :]
    tiles = row_tiles * col_tiles
    vmem = pl.BlockSpec(memory_space=pltpu.VMEM)
    tops, lefts = 2 * col_tiles * CHUNKS, 2 * row_tiles * CHUNKS
    new_u, new_v = pl.pallas_call(
        functools.partial(panels_kernel, row_size, col_size),
        out_shape=(
            jax.ShapeDtypeStruct(shape_four, BF16),
            jax.ShapeDtypeStruct(shape_four, BF16),
        ),
        in_specs=[pl.BlockSpec(memory_space=pltpu.SMEM)] + [vmem] * 6,
        out_specs=(vmem, vmem),
        scratch_shapes=[
            pltpu.VMEM((PANELS, 2, col_tiles, tile_size, rank_width), BF16),
            pltpu.VMEM((PANELS, 2, row_tiles, tile_size, rank_width), BF16),
            pltpu.VMEM((PANELS, tile_size, tile_size), BF16),
            pltpu.VMEM((col_tiles, tile_size, rank_width), BF16),
            pltpu.VMEM((row_tiles, tile_size, rank_width), BF16),
            pltpu.VMEM((tiles, tile_size, 2 * rank_width), BF16),
            pltpu.VMEM((tiles, rank_width, tile_size), F32),
            pltpu.SemaphoreType.DMA((PANELS, tops, 2)),
            pltpu.SemaphoreType.DMA((PANELS, tops)),
            pltpu.SemaphoreType.DMA((PANELS, lefts, 2)),
            pltpu.SemaphoreType.DMA((PANELS, lefts)),
        ],
        compiler_params=pltpu.CompilerParams(collective_id=0, has_side_effects=True),
        name="panels",
    )(ranks.reshape(-1), u, v, lower_inverse, upper_inverse, row_order, sketch)
    return new_u.reshape(tile_u.shape), new_v.reshape(tile_v.shape)


def solution(mesh):
    tile_spec = P(None, "row", None, "col", None, None)
    return jax.shard_map(
        functools.partial(on_device, mesh.shape["row"], mesh.shape["col"]),
        mesh=mesh,
        in_specs=(tile_spec, tile_spec, P(None, "row", None, "col"), P(), P(), P(), P()),
        out_specs=(tile_spec, tile_spec),
        check_vma=False,
    )
```
